32 devices in a mesh: tm: 4 (over y, core), scen: 8 (over z, x).
Axes of the slice: x: 2, y: 2, z: 4, core: 2. Of those that a mesh axis runs over, the one named last changes fastest.
Arguments:
- prior_dispatch: float32 [600, 8192], P(None, ('tm', 'scen')), may hold values from 0 to 1
- prior_commitment: float32 [600, 8192], P(None, ('tm', 'scen')), may hold values from 0 to 1
- prior_consensus: float32 [600, 32], P(None, 'tm'), may hold values from 0 to 1
- prior_multiplier: float32 [600, 8192], P(None, ('tm', 'scen')), may hold values from -2 to 2
- flow_factors: bfloat16 [2560, 2000], P('scen'), may hold values from -0.25 to 0.25
- unit_buses: int32 [600], replicated, may hold values from 0 to 1999
- wind_buses: int32 [128], replicated, may hold values from 0 to 1999
- wind_output: bfloat16 [128, 8192], P(None, ('tm', 'scen')), may hold values from 0 to 1
- demand: float32 [32], P('tm'), may hold values from 180 to 300
- load_flows: bfloat16 [2560, 32], P('scen', 'tm'), may hold values from -6 to 6
- line_limits: bfloat16 [2560], P('scen'), may hold values from 0.29882812 to 3
- unit_table: float32 [5, 600], replicated, may hold values from 0.05 to 2, as said below
Outputs:
- dispatch: float32 [600, 8192], P(None, ('tm', 'scen'))
- commitment: float32 [600, 8192], P(None, ('tm', 'scen'))
- consensus: float32 [600, 32], P(None, 'tm')
- multiplier: float32 [600, 8192], P(None, ('tm', 'scen'))
The draws below stay inside these ranges and needn't reach their ends.
Inputs may be any that keep to these rules, and one draw needn't show every extreme that they name: `unit_table`: rows 0 and 4 lie in 0.1 to 1, row 1 in 0.05 to 0.5, row 2 in 0.5 to 2, row 3 in 0.05 to 0.5.
All inputs are finite; a program needn't handle non-finite values.
Results may differ from the reference program's by a relative error of at most 0.0017.
Values may be sent and summed in bfloat16 or wider, within the bound.
A program may use at most 64 MiB of HBM per device.

```python
import math
import jax
import jax.numpy as jnp
from jax import lax

UNITS = 600
BUSES = 2000
LINES = 2560
FARMS = 128
PASSES = 3
H_DEV = 8
S_DEV = 32
HOURS = 32
SCENARIOS = 256
COLS = 8192
N_TM = 4
N_SCEN = 8


def draw_unit_table(key, part):
    keys = jax.random.split(jax.random.fold_in(key, 11), 5)
    linear = jax.random.uniform(keys[0], (UNITS,), jnp.float32, 0.1, 1.0)
    quadratic = jnp.exp(jax.random.uniform(keys[1], (UNITS,), jnp.float32, math.log(0.05), math.log(0.5)))
    capacity = jnp.exp(jax.random.uniform(keys[2], (UNITS,), jnp.float32, math.log(0.5), math.log(2.0)))
    ramp_limit = jnp.exp(jax.random.uniform(keys[3], (UNITS,), jnp.float32, math.log(0.05), math.log(0.5)))
    noload = jax.random.uniform(keys[4], (UNITS,), jnp.float32, 0.1, 1.0)
    return jnp.stack([linear, quadratic, capacity, ramp_limit, noload], axis=0)


def draw_prior_multiplier(key, part):
    keys = jax.random.split(jax.random.fold_in(key, 23), 2)
    offset = jax.random.uniform(keys[0], (UNITS, 1), jnp.float32, -1.5, 1.5)
    noise = jax.random.uniform(keys[1], (UNITS, COLS), jnp.float32, -0.5, 0.5)
    return offset + noise


def place_ends(values, own_key, low, largest):
    place = [jax.random.randint(jax.random.fold_in(own_key, axis), (), 0, length) for axis, length in enumerate(values.shape)]
    main_axis = values.shape.index(max(values.shape))
    beside = place[:main_axis] + [(place[main_axis] + 1) % values.shape[main_axis]] + place[main_axis + 1:]
    return values.at[tuple(place)].set(low).at[tuple(beside)].set(largest)


def block_scale(key, extent, cuts, least, largest):
    loudness, own = 1.0, jax.random.fold_in(key, 6)
    for dim, shards_of in cuts:
        steps = jnp.exp(jax.random.uniform(jax.random.fold_in(own, dim), (shards_of,), jnp.float32, least / len(cuts), largest / len(cuts)))
        loudness = loudness * jnp.repeat(steps, extent[dim] // shards_of).reshape([-1 if axis == dim else 1 for axis in range(len(extent))])
    return loudness


def gaussian(rng, shape, deviation, limit, shards=(), held_as=jnp.bfloat16):
    drawn = jax.random.normal(rng, shape, jnp.float32) * deviation
    if len(shards) > 0:
        drawn = block_scale(rng, shape, shards, -0.22, 0.18) * drawn
    return jnp.clip(drawn, min=-limit, max=limit).astype(held_as)


def setup_inputs(seed: int = 0) -> dict:
    streams_of = jax.random.split(jax.random.key(seed), 13)
    prior_dispatch = jnp.clip(1.0 * jax.random.uniform(streams_of[0], (UNITS, COLS), jnp.float32) ** block_scale(streams_of[0], (UNITS, COLS), ((1, 32),), -0.2, 0.2), 0.0, 1.0)
    prior_commitment = jnp.clip(1.0 * jax.random.uniform(streams_of[1], (UNITS, COLS), jnp.float32) ** block_scale(streams_of[1], (UNITS, COLS), ((1, 32),), -0.2, 0.2), 0.0, 1.0)
    prior_consensus = jnp.clip(1.0 * jax.random.uniform(streams_of[2], (UNITS, HOURS), jnp.float32) ** block_scale(streams_of[2], (UNITS, HOURS), ((1, 4),), -0.2, 0.2), 0.0, 1.0)
    prior_multiplier = draw_prior_multiplier(jax.random.fold_in(streams_of[12], 71), 0)
    flow_factors = gaussian(streams_of[4], (LINES, BUSES), UNITS ** -0.5, 0.25, ((0, 8),))
    unit_buses = place_ends(jax.random.randint(streams_of[5], (UNITS,), 0, BUSES), jax.random.fold_in(streams_of[5], 1), 0, BUSES - 1).astype(jnp.int32)
    wind_buses = place_ends(jax.random.randint(streams_of[6], (FARMS,), 0, BUSES), jax.random.fold_in(streams_of[6], 1), 0, BUSES - 1).astype(jnp.int32)
    wind_output = jnp.clip(1.0 * jax.random.uniform(streams_of[7], (FARMS, COLS), jnp.float32) ** block_scale(streams_of[7], (FARMS, COLS), ((1, 32),), -0.2, 0.2), 0.0, 1.0).astype(jnp.bfloat16)
    demand = jnp.clip(180.0 + 120.0 * jax.random.uniform(streams_of[8], (HOURS,), jnp.float32) ** block_scale(streams_of[8], (HOURS,), ((0, 4),), -0.2, 0.2), 180.0, 300.0)
    load_flows = gaussian(streams_of[9], (LINES, HOURS), 1.0, 6.0, ((0, 8), (1, 4)))
    line_limits = jnp.clip(jnp.exp(math.log(3.0) - 2.306499 * jax.random.uniform(streams_of[10], (LINES,), jnp.float32) ** block_scale(streams_of[10], (LINES,), ((0, 8),), -0.2, 0.2)), 0.29882812, 3.0).astype(jnp.bfloat16)
    unit_table = draw_unit_table(jax.random.fold_in(streams_of[12], 71), 0)
    return {"prior_dispatch": prior_dispatch, "prior_commitment": prior_commitment, "prior_consensus": prior_consensus, "prior_multiplier": prior_multiplier, "flow_factors": flow_factors, "unit_buses": unit_buses, "wind_buses": wind_buses, "wind_output": wind_output, "demand": demand, "load_flows": load_flows, "line_limits": line_limits, "unit_table": unit_table}


flow_weight = 0.5
ramp_weight = 1.0
balance_weight = 0.004
short_weight = 2.0
penalty = 1.0
step_power = 0.2
step_commit = 0.3


def to_grid(array):
    rows = array.shape[0]
    array = array.reshape(rows, N_TM, N_SCEN, H_DEV, S_DEV).transpose(0, 1, 3, 2, 4)
    return array.reshape(rows, HOURS, SCENARIOS)


def from_grid(array):
    rows = array.shape[0]
    array = array.reshape(rows, N_TM, H_DEV, N_SCEN, S_DEV).transpose(0, 1, 3, 2, 4)
    return array.reshape(rows, COLS)


def reference(prior_dispatch, prior_commitment, prior_consensus, prior_multiplier, flow_factors, unit_buses, wind_buses, wind_output, demand, load_flows, line_limits, unit_table):
    linear = unit_table[0][:, None, None]
    quadratic = unit_table[1][:, None, None]
    capacity = unit_table[2][:, None, None]
    ramp_limit = unit_table[3][:, None, None]
    noload = unit_table[4][:, None, None]
    factors = jnp.concatenate([flow_factors[:, unit_buses], flow_factors[:, wind_buses]], axis=1)
    gen_factors = factors[:, :UNITS]
    power = to_grid(prior_dispatch)
    commit = to_grid(prior_commitment)
    multiplier = to_grid(prior_multiplier)
    wind = to_grid(wind_output)
    wind_hours = wind.transpose(1, 0, 2)
    wind_total = jnp.sum(wind.astype(jnp.float32), axis=0)
    target = prior_consensus[:, :, None]
    hourly = load_flows.astype(jnp.float32).T
    bounds = line_limits.astype(jnp.float32)[:, None]

    def per_hour(items):
        power_hour, wind_hour, load_hour = items
        extended = jnp.concatenate([power_hour, wind_hour], axis=0)
        flows = jnp.dot(factors, extended, preferred_element_type=jnp.float32) - load_hour[:, None]
        excess = flows - jnp.clip(flows, -bounds, bounds)
        return jnp.dot(gen_factors.T, excess.astype(jnp.bfloat16), preferred_element_type=jnp.float32)

    for number in range(PASSES):
        rounded = power.astype(jnp.bfloat16).transpose(1, 0, 2)
        back = lax.map(per_hour, (rounded, wind_hours, hourly)).transpose(1, 0, 2)
        previous = jnp.concatenate([power[:, :1], power[:, :-1]], axis=1)
        rate = power - previous
        over = rate - jnp.clip(rate, -ramp_limit, ramp_limit)
        following = jnp.concatenate([over[:, 1:], jnp.zeros_like(over[:, :1])], axis=1)
        ramp_term = over - following
        balance = jnp.sum(power, axis=0) + wind_total - demand[:, None]
        short = jnp.maximum(power - capacity * commit, 0.0)
        grad_power = linear + 2.0 * quadratic * power + flow_weight * back + ramp_weight * ramp_term + balance_weight * balance + short_weight * short
        grad_commit = noload - short_weight * capacity * short + multiplier + penalty * (commit - target)
        power = jnp.clip(power - step_power * grad_power, 0.0, capacity)
        commit = jnp.clip(commit - step_commit * grad_commit, 0.0, 1.0)
    consensus = jnp.clip(jnp.sum(commit + multiplier / penalty, axis=2) / SCENARIOS, 0.0, 1.0)
    updated = multiplier + penalty * (commit - consensus[:, :, None])
    return from_grid(power), from_grid(commit), consensus, from_grid(updated)
```

```python
import functools

import jax
import jax.numpy as jnp
from jax import lax
from jax.experimental import pallas as pl
from jax.experimental.pallas import tpu as pltpu
from jax.sharding import PartitionSpec as P

PASSES = 3
H_DEV = 8
MESH = pl.DeviceIdType.MESH

flow_weight = 0.5
ramp_weight = 1.0
balance_weight = 0.004
short_weight = 2.0
penalty = 1.0
step_power = 0.2
step_commit = 0.3


def split(value):
    high = value.astype(jnp.bfloat16)
    rest = value - high.astype(jnp.float32)
    middle = rest.astype(jnp.bfloat16)
    return high, middle, (rest - middle.astype(jnp.float32)).astype(jnp.bfloat16)


def beyond(value, limit):
    return value - jnp.minimum(jnp.maximum(value, -limit), limit)


def kernel(n_tm, n_scen, units, fl_hbm, pd_hbm, pc_hbm, mu_hbm, wind_hbm, ub_ref, wb_ref, tab_ref, lim_ref, cons_ref,
           table_ref, need_ref,
           power_out, commit_out, mult_out, cons_out,
           fbuf, hot, ids, fac, fact, load, bound, exc, pw, cm, mult, off, part, ext, backs, bef, aft,
           keep, lin, cap, ramp, tabs, esend, erecv, psend, precv, wind_row, small,
           in_sem, out_sem, recv_sem, zsend, xsend, ysend, csend, tsend, trecv, esem_s, esem_r, psem_s, psem_r):
    rows, buses = fbuf.shape
    quarter = rows // 4
    up, cols = pw.shape
    half = cols // 2
    block = cols // H_DEV
    chunk = 2 * rows
    n_z = n_scen // 2
    f32, bf16 = jnp.float32, jnp.bfloat16
    tm = lax.axis_index("tm")
    scen = lax.axis_index("scen")
    y, c = tm // 2, tm % 2
    z, x = scen // 2, scen % 2
    oy = 1 - y
    oc = 1 - c
    ox = 1 - x
    mine = y * 2 + c
    other = oy * 2 + c
    dev_x = (tm, z * 2 + ox)
    dev_y = (oy * 2 + c, scen)
    dev_c = (y * 2 + oc, scen)

    load_in = [pltpu.make_async_copy(src, dst, in_sem.at[i]) for i, (src, dst) in enumerate((
        (fl_hbm, fbuf), (pd_hbm, pw.at[pl.ds(0, units), :]), (pc_hbm, cm.at[pl.ds(0, units), :]),
        (mu_hbm, mult.at[pl.ds(0, units), :]), (wind_hbm, ext.at[pl.ds(up, wind_hbm.shape[0]), :])))]
    for item in load_in:
        item.start()

    barrier = pltpu.get_barrier_semaphore()
    for k in range(1, n_scen):
        pl.semaphore_signal(barrier, inc=1, device_id=(tm, lax.rem(scen + k, n_scen)), device_id_type=MESH)
    for k in range(1, n_tm):
        pl.semaphore_signal(barrier, inc=1, device_id=(lax.rem(tm + k, n_tm), scen), device_id_type=MESH)

    first_rows = -(-quarter // 32) * 16
    starts = (0, first_rows)
    sizes = (first_rows, quarter - first_rows)

    def piece(zz, xx, q):
        return (zz * 2 + xx) * 4 + q

    def copy(p, h, sem, dev):
        ref = fac.at[pl.ds(pl.multiple_of(p * quarter + starts[h], 16), sizes[h]), :]
        return pltpu.make_async_remote_copy(
            src_ref=ref, dst_ref=ref, send_sem=sem, recv_sem=recv_sem.at[h, p],
            device_id=dev, device_id_type=MESH)

    def to_z(p, h, way):
        return copy(p, h, zsend.at[way, h, p], (tm, scen + 2 * (2 * way - 1)))

    def to_x(p, h):
        return copy(p, h, xsend.at[h, p], dev_x)

    def to_y(p, h):
        return copy(p, h, ysend.at[h, p], dev_y)

    def to_c(p, h):
        return copy(p, h, csend.at[h, p], dev_c)

    def arrived(p, h):
        to_x(p, h).wait_recv()

    def table_copy(k):
        peer = lax.rem(scen + k, n_scen)
        return pltpu.make_async_remote_copy(
            src_ref=tabs.at[scen], dst_ref=tabs.at[scen], send_sem=tsend.at[k], recv_sem=trecv.at[scen],
            device_id=(tm, peer), device_id_type=MESH)

    ids[...] = jnp.full(ids.shape, -1, jnp.int32)
    ids[0:1, :units] = ub_ref[...].reshape(1, units)
    ids[0:1, up:] = wb_ref[...].reshape(1, ids.shape[1] - up)
    step = 256
    number = lax.broadcasted_iota(jnp.int32, (step, ids.shape[1]), 0).astype(f32).astype(bf16)
    wanted = ids[0:1, :]
    one = jnp.ones((), bf16)
    for k in range(0, buses, step):
        here = jnp.where((wanted >= k) & (wanted < k + step), wanted - k, -1).astype(f32).astype(bf16)
        n = min(step, buses - k)
        hot[k:k + n, :] = jnp.where(number[:n] == here, one, one - one)
    tabs[scen] = jnp.concatenate(
        [tab_ref[...].astype(f32), jnp.broadcast_to(lim_ref[...].astype(f32).reshape(1, rows), (8, rows))], axis=0).astype(bf16)
    load_in[0].wait()

    def select(part_of):
        src = pl.ds(pl.multiple_of(part_of * 2 * quarter, 16), 2 * quarter)
        dst = pl.ds(pl.multiple_of(scen * rows + part_of * 2 * quarter, 16), 2 * quarter)
        fac[dst, :] = jnp.dot(fbuf[src, :], hot[...], preferred_element_type=f32).astype(bf16)

    select(y)
    pl.semaphore_wait(barrier, n_scen - 1 + n_tm - 1)

    p_own = piece(z, x, mine)

    def own_sends(f):
        for h in range(2):
            f(to_x(p_own, h))

            @pl.when(z > 0)
            def _():
                f(to_z(p_own, h, 0))

            @pl.when(z < n_z - 1)
            def _():
                f(to_z(p_own, h, 1))

    own_sends(lambda item: item.start())
    for k in range(1, n_scen):
        table_copy(k).start()

    def edges_of(tile_last, tile_first):
        lane = lax.broadcasted_iota(jnp.int32, (up // 4, 128), 1)
        last = jnp.zeros((up // 4, 128), f32)
        first = jnp.zeros((up // 4, 128), f32)
        for g in range(4):
            inside = (lane >= 32 * g) & (lane < 32 * g + 32)
            a = tile_last[g * (up // 4):(g + 1) * (up // 4), :]
            b = tile_first[g * (up // 4):(g + 1) * (up // 4), :]
            sa = (32 * g - 96) % 128
            sb = (32 * g) % 128
            a = pltpu.roll(a, sa, 1) if sa else a
            b = pltpu.roll(b, sb, 1) if sb else b
            last = jnp.where(inside, a, last)
            first = jnp.where(inside, b, first)
        return last, first

    def edge_copy(number, way):
        dev = (tm + 1, scen) if way == 0 else (tm - 1, scen)
        return pltpu.make_async_remote_copy(
            src_ref=esend.at[number, way], dst_ref=erecv.at[number, way],
            send_sem=esem_s.at[number, way], recv_sem=esem_r.at[number, way],
            device_id=dev, device_id_type=MESH)

    def send_edges(number):
        last, first = edges_of(pw[:, cols - 128:], pw[:, :128])
        esend[number, 0] = last
        esend[number, 1] = first

        @pl.when(tm < n_tm - 1)
        def _():
            edge_copy(number, 0).start()

        @pl.when(tm > 0)
        def _():
            edge_copy(number, 1).start()

    def take_edges(number):
        @pl.when(tm > 0)
        def _():
            edge_copy(number, 0).wait_recv()
            e = erecv[number, 0]
            for g in range(4):
                s = (-32 * g) % 128
                bef[g * (up // 4):(g + 1) * (up // 4), :] = pltpu.roll(e, s, 1) if s else e

        @pl.when(tm == 0)
        def _():
            bef[...] = pw[:, :128]

        @pl.when(tm < n_tm - 1)
        def _():
            edge_copy(number, 1).wait_recv()
            e = erecv[number, 1]
            for g in range(4):
                s = (96 - 32 * g) % 128
                aft[g * (up // 4):(g + 1) * (up // 4), :] = pltpu.roll(e, s, 1) if s else e

        @pl.when(tm == n_tm - 1)
        def _():
            aft[...] = pw[:, cols - 128:]

    for item in load_in[1:]:
        item.wait()
    tail = jnp.zeros((up - units, cols), f32)
    pw[units:, :] = tail
    cm[units:, :] = tail
    mult[units:, :] = tail
    send_edges(0)
    select(oy)

    hour_row = lax.broadcasted_iota(jnp.int32, (2 * H_DEV, cols), 0)
    hour_col = lax.broadcasted_iota(jnp.int32, (2 * H_DEV, cols), 1)
    hour_of = ((hour_col >= hour_row * block) & (hour_col < hour_row * block + block)).astype(f32)
    load_of = hour_of.astype(bf16)
    bound_of = (hour_row == H_DEV).astype(f32).astype(bf16)
    lines_first = (((0,), (0,)), ((), ()))

    small[...] = jnp.zeros_like(small)
    small[:, :units] = cons_ref[...]
    target = jnp.dot(small[...].T, hour_of[:H_DEV], preferred_element_type=f32, precision=lax.Precision.HIGHEST)
    small[...] = jnp.zeros_like(small)
    small[:table_ref.shape[0], :units] = table_ref[...]
    table = small[...].T
    keep[...] = jnp.broadcast_to(1.0 - 2.0 * step_power * table[:, 1:2], keep.shape)
    lin[...] = jnp.broadcast_to(step_power * table[:, 0:1], lin.shape)
    cap[...] = jnp.broadcast_to(table[:, 2:3], cap.shape)
    ramp[...] = jnp.broadcast_to(table[:, 3:4], ramp.shape)
    off[...] = step_commit * (table[:, 4:5] + mult[...] - penalty * target)
    ext[:up, :] = pw[...].astype(bf16)
    needed = jnp.zeros((1, cols), f32)
    for h in range(H_DEV):
        needed = jnp.where(hour_of[h:h + 1] > 0.0, need_ref[h], needed)
    wind_row[...] = jnp.sum(ext[up:, :].astype(f32), axis=0, keepdims=True) - needed
    backs[...] = jnp.zeros((up, cols), f32)

    tile = 32
    lane = lax.broadcasted_iota(jnp.int32, (tile, half), 1)

    def start_next(r, p, both):
        capacity = cap[r, :]
        for i in range(2):
            h = pl.ds(i * half, half)
            commit = cm[r, h]
            short = jnp.maximum(p[i] - capacity * commit, 0.0)
            part[r, h] = p[i] * keep[r, :] - lin[r, :] - (step_power * short_weight) * short
            cm[r, h] = jnp.clip((1.0 - step_commit * penalty) * commit - off[r, h]
                                + (step_commit * short_weight) * capacity * short, 0.0, 1.0)

    def first_part(i, total):
        r = pl.ds(pl.multiple_of(i * tile, tile), tile)
        p = (pw[r, :half], pw[r, half:])
        start_next(r, p, True)
        both = jnp.concatenate(p, axis=1)
        return total + sum(both[8 * j:8 * j + 8] for j in range(tile // 8))

    def add_ramp(balance):
        for i in range(up // tile):
            r = pl.ds(i * tile, tile)
            p0, p1 = pw[r, :half], pw[r, half:]
            limit = ramp[r, :]
            r0, r1 = pltpu.roll(p0, block, 1), pltpu.roll(p1, block, 1)
            o0 = beyond(p0 - jnp.where(lane < block, bef[r, :], r0), limit)
            o1 = beyond(p1 - jnp.where(lane < block, r0, r1), limit)
            o2 = beyond(aft[r, :] - p1, limit)
            s0, s1 = pltpu.roll(o0, half - block, 1), pltpu.roll(o1, half - block, 1)
            f0 = jnp.where(lane >= half - block, s1, s0)
            f1 = jnp.where(lane >= half - block, o2, s1)
            part[r, :half] = part[r, :half] - (step_power * ramp_weight) * (o0 - f0) - balance[:, :half]
            part[r, half:] = part[r, half:] - (step_power * ramp_weight) * (o1 - f1) - balance[:, half:]

    def settle(last):
        def body(i, total):
            r = pl.ds(pl.multiple_of(i * tile, tile), tile)
            capacity = cap[r, :]
            p = []
            for j in range(2):
                h = pl.ds(j * half, half)
                p.append(jnp.minimum(jnp.maximum(part[r, h] - (step_power * flow_weight) * backs[r, h], 0.0), capacity))
                if last:
                    power_out_tile(r, h, p[j])
                else:
                    pw[r, h] = p[j]
                    ext[r, h] = p[j].astype(bf16)
            if last:
                return total
            start_next(r, p, True)
            both = jnp.concatenate(p, axis=1)
            return total + sum(both[8 * j:8 * j + 8] for j in range(tile // 8))
        return lax.fori_loop(0, up // tile, body, jnp.zeros((8, cols), f32), unroll=2)

    def power_out_tile(r, h, value):
        pw[r, h] = value

    def balance_of(total):
        return (step_power * balance_weight) * (jnp.sum(total, axis=0, keepdims=True) + wind_row[...])

    total = lax.fori_loop(0, up // tile, first_part, jnp.zeros((8, cols), f32), unroll=2)

    def line_step(at_rows):
        flows = jnp.dot(fac[at_rows, :], ext[...], preferred_element_type=f32) - load[at_rows, :]
        exc[at_rows, :] = beyond(flows, bound[at_rows, :]).astype(bf16)

    def process(zz):
        for xx in range(2):
            s = zz * 2 + xx
            at_rows = pl.ds(pl.multiple_of(s * rows, 16), rows)
            load[at_rows, :] = lax.dot_general(tabs[s], load_of, lines_first, preferred_element_type=f32)
            bound[at_rows, :] = lax.dot_general(tabs[s], bound_of, lines_first, preferred_element_type=f32)
        at_rows = pl.ds(pl.multiple_of(zz * chunk, 128), chunk)
        fact[:, at_rows] = fac[at_rows, :up].T
        line_step(at_rows)
        backs[...] += jnp.dot(fact[:, at_rows], exc[at_rows, :], preferred_element_type=f32)

    def table_arrived(src):
        pltpu.make_async_remote_copy(
            src_ref=tabs.at[src], dst_ref=tabs.at[src], send_sem=tsend.at[0], recv_sem=trecv.at[src],
            device_id=dev_x, device_id_type=MESH).wait_recv()

    def both(k, f, *rest):
        if k >= n_z:
            return

        @pl.when(z - k >= 0)
        def _():
            f(z - k, *rest)

        @pl.when(z + k < n_z)
        def _():
            f(z + k, *rest)

    def from_z(k, h):
        if k >= n_z:
            return
        for way in range(2):
            zz = z - k if way else z + k

            @pl.when(zz >= 0 if way else zz < n_z)
            def _():
                p = piece(zz, x, mine)
                arrived(p, h)

                @pl.when(z < n_z - 1 if way else z > 0)
                def _():
                    to_z(p, h, way).start()
                to_x(p, h).start()
                to_y(p, h).start()
                to_c(p, h).start()

    def from_xy(zz, h):
        p = piece(zz, ox, mine)
        arrived(p, h)

        @pl.when(c == 0)
        def _():
            to_y(p, h).start()
        to_c(p, h).start()
        p = piece(zz, x, other)
        arrived(p, h)

        @pl.when(c == 1)
        def _():
            to_x(p, h).start()
        to_c(p, h).start()

    def from_corner(zz, h):
        p = piece(zz, ox, other)
        arrived(p, h)
        to_c(p, h).start()

    def own_x(h):
        p = piece(z, ox, mine)
        arrived(p, h)
        to_y(p, h).start()
        to_c(p, h).start()

    def from_core(zz):
        for xx in range(2):
            for yy in range(2):
                for h in range(2):
                    arrived(piece(zz, xx, yy * 2 + oc), h)
            table_arrived(zz * 2 + xx)
        process(zz)

    def own_chunk():
        for q in (oc, 2 + oc):
            for h in range(2):
                arrived(piece(z, ox, q), h)
        table_arrived(z * 2 + ox)
        process(z)

    for h in range(2):
        own_x(h)
        from_z(1, h)
    take_edges(0)
    add_ramp(balance_of(total))
    for k in range(2, n_z + 2):
        for h in range(2):
            from_z(k, h)
            if k == 2:
                from_corner(z, h)
            both(k - 1, from_xy, h)
            if k > 2:
                both(k - 2, from_corner, h)
        if k == 3:
            own_chunk()
        if k > 3:
            both(k - 3, from_core)
    both(n_z - 1, from_core)

    total = settle(False)
    spread = hour_of[:H_DEV].astype(bf16)

    def sum_copy(k):
        return pltpu.make_async_remote_copy(
            src_ref=psend, dst_ref=precv.at[scen], send_sem=psem_s.at[k], recv_sem=psem_r.at[scen],
            device_id=(tm, lax.rem(scen + k, n_scen)), device_id_type=MESH)

    def put(i, src, dst):
        return pltpu.make_async_copy(src, dst, out_sem.at[i])

    put_commit = put(0, cm.at[pl.ds(0, units), :], commit_out)
    put_mult = put(1, mult.at[pl.ds(0, units), :], mult_out)
    put_power = put(2, pw.at[pl.ds(0, units), :], power_out)
    for number in range(1, PASSES):
        send_edges(number)
        final = number == PASSES - 1
        if final:
            put_commit.start()
            sums = jnp.zeros((H_DEV, up), f32)
            for item in split(cm[...] + mult[...] / penalty):
                sums = sums + lax.dot_general(spread, item, (((1,), (1,)), ((), ())), preferred_element_type=f32)
            psend[...] = sums
            for k in range(1, n_scen):
                sum_copy(k).start()
        for k in range(n_z):
            line_step(pl.ds(k * chunk, chunk))
        take_edges(number)
        add_ramp(balance_of(total))
        backs[...] = jnp.dot(fact[...], exc[...], preferred_element_type=f32)
        if final:
            precv[scen] = psend[...]
            for k in range(1, n_scen):
                src = lax.rem(scen + k, n_scen)
                pltpu.make_async_remote_copy(
                    src_ref=psend, dst_ref=precv.at[src], send_sem=psem_s.at[k], recv_sem=psem_r.at[src],
                    device_id=dev_x, device_id_type=MESH).wait_recv()
            totals = precv[0]
            for k in range(1, n_scen):
                totals = totals + precv[k]
            consensus = jnp.clip(totals / (block * n_scen), 0.0, 1.0)
            cons_out[...] = consensus[:, :units]
            pieces = jnp.concatenate([item.astype(f32) for item in split(consensus)], axis=0).T.astype(bf16)
            three = jnp.concatenate([hour_of[:H_DEV]] * 3, axis=0).astype(bf16)
            wide = jnp.dot(pieces, three, preferred_element_type=f32)
            mult[...] = mult[...] + penalty * (cm[...] - wide)
            put_mult.start()
        total = settle(final)
    put_power.start()

    own_sends(lambda item: item.wait_send())
    for h in range(2):
        p = piece(z, ox, mine)
        to_y(p, h).wait_send()
        to_c(p, h).wait_send()
        to_c(piece(z, ox, other), h).wait_send()

    def drain(k, way):
        zz = z - k if way else z + k

        @pl.when(zz >= 0 if way else zz < n_z)
        def _():
            for h in range(2):
                p = piece(zz, x, mine)

                @pl.when(z < n_z - 1 if way else z > 0)
                def _():
                    to_z(p, h, way).wait_send()
                to_x(p, h).wait_send()
                to_y(p, h).wait_send()
                to_c(p, h).wait_send()
                to_c(piece(zz, ox, mine), h).wait_send()
                to_c(piece(zz, x, other), h).wait_send()
                to_c(piece(zz, ox, other), h).wait_send()

                @pl.when(c == 0)
                def _():
                    to_y(piece(zz, ox, mine), h).wait_send()

                @pl.when(c == 1)
                def _():
                    to_x(piece(zz, x, other), h).wait_send()

    for k in range(1, n_z):
        for way in range(2):
            drain(k, way)
    for k in range(1, n_scen):
        table_copy(k).wait_send()
        sum_copy(k).wait_send()
    put_commit.wait()
    put_mult.wait()
    put_power.wait()
    for number in range(PASSES):
        @pl.when(tm < n_tm - 1)
        def _():
            edge_copy(number, 0).wait_send()

        @pl.when(tm > 0)
        def _():
            edge_copy(number, 1).wait_send()


def selection(unit_buses, wind_buses, buses, up, dtype):
    units = unit_buses.shape[0]
    wanted = jnp.concatenate([unit_buses, jnp.full((up - units,), -1, unit_buses.dtype), wind_buses])
    return (lax.broadcasted_iota(jnp.int32, (buses, wanted.shape[0]), 0) == wanted[None, :]).astype(dtype)


def finish(power_ref, commit_ref, mult_ref, cons_ref, power_out, commit_out, mult_out, cons_out):
    power_out[...] = power_ref[...]
    commit_out[...] = commit_ref[...]
    mult_out[...] = mult_ref[...]
    cons_out[...] = cons_ref[...]


def fused(n_tm, n_scen, prior_dispatch, prior_commitment, prior_consensus, prior_multiplier, flow_factors,
          unit_buses, wind_buses, wind_output, demand, load_flows, line_limits, unit_table):
    units, cols = prior_dispatch.shape
    rows, buses = flow_factors.shape
    farms = wind_output.shape[0]
    up = -(-units // 128) * 128
    f32, bf16 = jnp.float32, jnp.bfloat16
    lines = rows * n_scen
    wide = up + farms
    vm = pl.BlockSpec(memory_space=pltpu.VMEM)
    hbm = pl.BlockSpec(memory_space=pl.ANY)
    dma = pltpu.SemaphoreType.DMA
    shapes = (
        jax.ShapeDtypeStruct((units, cols), f32),
        jax.ShapeDtypeStruct((units, cols), f32),
        jax.ShapeDtypeStruct((units, cols), f32),
        jax.ShapeDtypeStruct((H_DEV, units), f32),
    )
    outs = pl.pallas_call(
        functools.partial(kernel, n_tm, n_scen, units),
        name="window",
        out_shape=shapes,
        in_specs=[hbm] * 5 + [vm] * 6 + [pl.BlockSpec(memory_space=pltpu.SMEM)],
        out_specs=(hbm, hbm, hbm, vm),
        scratch_shapes=[
            pltpu.VMEM((rows, buses), bf16),
            pltpu.VMEM((buses, wide), bf16),
            pltpu.VMEM((8, wide), jnp.int32),
            pltpu.VMEM((lines, wide), bf16),
            pltpu.VMEM((up, lines), bf16),
            pltpu.VMEM((lines, cols), f32),
            pltpu.VMEM((lines, cols), f32),
            pltpu.VMEM((lines, cols), bf16),
            pltpu.VMEM((up, cols), f32),
            pltpu.VMEM((up, cols), f32),
            pltpu.VMEM((up, cols), f32),
            pltpu.VMEM((up, cols), f32),
            pltpu.VMEM((up, cols), f32),
            pltpu.VMEM((wide, cols), bf16),
            pltpu.VMEM((up, cols), f32),
            pltpu.VMEM((up, 128), f32),
            pltpu.VMEM((up, 128), f32),
            pltpu.VMEM((up, 128), f32),
            pltpu.VMEM((up, 128), f32),
            pltpu.VMEM((up, 128), f32),
            pltpu.VMEM((up, 128), f32),
            pltpu.VMEM((n_scen, 2 * H_DEV, rows), bf16),
            pltpu.VMEM((PASSES, 2, up // 4, 128), f32),
            pltpu.VMEM((PASSES, 2, up // 4, 128), f32),
            pltpu.VMEM((H_DEV, up), f32),
            pltpu.VMEM((n_scen, H_DEV, up), f32),
            pltpu.VMEM((1, cols), f32),
            pltpu.VMEM((H_DEV, up), f32),
            dma((5,)),
            dma((3,)),
            dma((2, n_scen * 4)),
            dma((2, 2, n_scen * 4)),
            dma((2, n_scen * 4)),
            dma((2, n_scen * 4)),
            dma((2, n_scen * 4)),
            dma((n_scen,)),
            dma((n_scen,)),
            dma((PASSES, 2)),
            dma((PASSES, 2)),
            dma((n_scen,)),
            dma((n_scen,)),
        ],
        compiler_params=pltpu.CompilerParams(collective_id=0, has_side_effects=True, vmem_limit_bytes=56 * 1024 * 1024),
    )(flow_factors, prior_dispatch, prior_commitment, prior_multiplier, wind_output,
      unit_buses, wind_buses, load_flows.T, line_limits,
      prior_consensus.T, unit_table, demand)
    power, commit, updated, cons = pl.pallas_call(
        finish,
        name="finish",
        out_shape=shapes,
        in_specs=[vm] * 4,
        out_specs=(vm,) * 4,
    )(*outs)
    return power, commit, cons.T, updated


def passed_along(value, axis, steps):
    count = lax.axis_size(axis)
    first, last = (max(0, -steps), min(count, count - steps))
    return lax.ppermute(value, axis, [(source, source + steps) for source in range(first, last)])


def plain(prior_dispatch, prior_commitment, prior_consensus, prior_multiplier, flow_factors,
          unit_buses, wind_buses, wind_output, demand, load_flows, line_limits, unit_table):
    units, columns = prior_dispatch.shape
    block = columns // H_DEV
    linear, quadratic, capacity, ramp_limit, noload = (unit_table[i][:, None] for i in range(5))
    factors = jnp.dot(flow_factors, selection(unit_buses, wind_buses, flow_factors.shape[1], units, jnp.bfloat16),
                      preferred_element_type=jnp.float32).astype(jnp.bfloat16)
    wind_total = jnp.sum(wind_output.astype(jnp.float32), axis=0)
    needed = jnp.repeat(demand, block)
    target = jnp.repeat(prior_consensus, block, axis=1)
    first_block = lax.axis_index("tm") == 0
    last_block = lax.axis_index("tm") == lax.axis_size("tm") - 1
    power, commit = prior_dispatch, prior_commitment
    factors = lax.all_gather(factors, "scen", axis=0, tiled=True)
    hourly = jnp.repeat(lax.all_gather(load_flows, "scen", axis=0, tiled=True).astype(jnp.float32), block, axis=1)
    limit = lax.all_gather(line_limits, "scen", axis=0, tiled=True).astype(jnp.float32)[:, None]
    for _ in range(PASSES):
        extended = jnp.concatenate([power.astype(jnp.bfloat16), wind_output], axis=0)
        flows = jnp.dot(factors, extended, preferred_element_type=jnp.float32) - hourly
        excess = (flows - jnp.clip(flows, -limit, limit)).astype(jnp.bfloat16)
        back = lax.dot_general(factors[:, :units], excess, (((0,), (0,)), ((), ())), preferred_element_type=jnp.float32)
        before = passed_along(power[:, columns - block:], "tm", 1)
        after = passed_along(power[:, :block], "tm", -1)
        before = jnp.where(first_block, power[:, :block], before)
        after = jnp.where(last_block, power[:, columns - block:], after)
        rate = power - jnp.concatenate([before, power[:, :columns - block]], axis=1)
        coming = jnp.concatenate([power[:, block:], after], axis=1) - power
        over = rate - jnp.clip(rate, -ramp_limit, ramp_limit)
        following = coming - jnp.clip(coming, -ramp_limit, ramp_limit)
        balance = jnp.sum(power, axis=0) + wind_total - needed
        short = jnp.maximum(power - capacity * commit, 0.0)
        grad_power = (linear + 2.0 * quadratic * power + flow_weight * back + ramp_weight * (over - following)
                      + balance_weight * balance + short_weight * short)
        grad_commit = noload - short_weight * capacity * short + prior_multiplier + penalty * (commit - target)
        power, commit = (jnp.clip(power - step_power * grad_power, 0.0, capacity),
                         jnp.clip(commit - step_commit * grad_commit, 0.0, 1.0))
    sums = jnp.sum((commit + prior_multiplier / penalty).reshape(units, H_DEV, block), axis=2)
    totals = lax.psum(sums, "scen")
    consensus = jnp.clip(totals / (block * lax.axis_size("scen")), 0.0, 1.0)
    updated = prior_multiplier + penalty * (commit - jnp.repeat(consensus, block, axis=1))
    return power, commit, consensus, updated


def solution(mesh):
    n_tm, n_scen = mesh.shape["tm"], mesh.shape["scen"]

    def per_device(*args):
        rows, cols = args[4].shape[0], args[0].shape[1]
        fits = (n_tm == 4 and n_scen % 2 == 0 and rows % 64 == 0 and cols == 256
                and args[7].shape[0] % 128 == 0 and args[0].shape[0] % 128 > 0)
        if fits:
            return fused(n_tm, n_scen, *args)
        return plain(*args)

    both_axes = P(None, ("tm", "scen"))
    in_specs = (both_axes, both_axes, P(None, "tm"), both_axes, P("scen", None), P(), P(), both_axes,
                P("tm"), P("scen", "tm"), P("scen"), P())
    out_specs = (both_axes, both_axes, P(None, "tm"), both_axes)
    return jax.shard_map(per_device, mesh=mesh, in_specs=in_specs, out_specs=out_specs, check_vma=False)
```

```python
import functools

import jax
import jax.numpy as jnp
from jax import lax
from jax.experimental import pallas as pl
from jax.experimental.pallas import tpu as pltpu
from jax.sharding import PartitionSpec as P

PASSES = 3
H_DEV = 8
MESH = pl.DeviceIdType.MESH

flow_weight = 0.5
ramp_weight = 1.0
balance_weight = 0.004
short_weight = 2.0
penalty = 1.0
step_power = 0.2
step_commit = 0.3


def split(value):
    high = value.astype(jnp.bfloat16)
    rest = value - high.astype(jnp.float32)
    middle = rest.astype(jnp.bfloat16)
    return high, middle, (rest - middle.astype(jnp.float32)).astype(jnp.bfloat16)


def beyond(value, limit):
    return value - jnp.minimum(jnp.maximum(value, -limit), limit)


def kernel(n_tm, n_scen, units, fl_hbm, pd_hbm, pc_hbm, mu_hbm, wind_hbm, ub_ref, wb_ref, tab_ref, lim_ref, cons_ref,
           table_ref, need_ref,
           power_out, commit_out, mult_out, cons_out,
           fbuf, hot, ids, fac, fact, load, bound, exc, pw, cm, mult, off, part, ext, backs, bef, aft,
           keep, lin, cap, ramp, tabs, esend, erecv, psend, precv, wind_row, small,
           in_sem, out_sem, recv_sem, crecv, zsend, xsend, ysend, csend, tsend, trecv, esem_s, esem_r, psem_s, psem_r):
    rows, buses = fbuf.shape
    quarter = rows // 4
    up, cols = pw.shape
    half = cols // 2
    block = cols // H_DEV
    chunk = 2 * rows
    n_z = n_scen // 2
    f32, bf16 = jnp.float32, jnp.bfloat16
    tm = lax.axis_index("tm")
    scen = lax.axis_index("scen")
    y, c = tm // 2, tm % 2
    z, x = scen // 2, scen % 2
    oy = 1 - y
    oc = 1 - c
    ox = 1 - x
    mine = y * 2 + c
    other = oy * 2 + c
    dev_x = (tm, z * 2 + ox)
    dev_y = (oy * 2 + c, scen)
    dev_c = (y * 2 + oc, scen)

    load_in = [pltpu.make_async_copy(src, dst, in_sem.at[i]) for i, (src, dst) in enumerate((
        (fl_hbm, fbuf), (pd_hbm, pw.at[pl.ds(0, units), :]), (pc_hbm, cm.at[pl.ds(0, units), :]),
        (mu_hbm, mult.at[pl.ds(0, units), :]), (wind_hbm, ext.at[pl.ds(up, wind_hbm.shape[0]), :])))]
    for item in load_in:
        item.start()

    barrier = pltpu.get_barrier_semaphore()
    for k in range(1, n_scen):
        pl.semaphore_signal(barrier, inc=1, device_id=(tm, lax.rem(scen + k, n_scen)), device_id_type=MESH)
    for k in range(1, n_tm):
        pl.semaphore_signal(barrier, inc=1, device_id=(lax.rem(tm + k, n_tm), scen), device_id_type=MESH)

    first_rows = -(-quarter // 32) * 16
    starts = (0, first_rows, 0)
    sizes = (first_rows, quarter - first_rows, quarter)
    whole = 2

    def piece(zz, xx, q):
        return (zz * 2 + xx) * 4 + q

    def copy(p, h, sem, dev, got=None):
        ref = fac.at[pl.ds(pl.multiple_of(p * quarter + starts[h], 16), sizes[h]), :]
        return pltpu.make_async_remote_copy(
            src_ref=ref, dst_ref=ref, send_sem=sem, recv_sem=recv_sem.at[h % 2, p // 8 * 4 + p // 4 % 2 * 2 + p % 4 // 2] if got is None else got,
            device_id=dev, device_id_type=MESH)

    def to_z(p, h, way):
        return copy(p, h, zsend.at[way, p // 8], (tm, scen + 2 * (2 * way - 1)))

    def to_x(p, h):
        return copy(p, h, xsend.at[p // 8 * 2 + (p % 4) // 2 * y + (1 - (p % 4) // 2) * (1 - y)], dev_x)

    def to_y(p, h):
        return copy(p, h, ysend.at[p // 4], dev_y)

    def to_c(p, h):
        return copy(p, h, csend.at[p // 2], dev_c, crecv.at[p // 2])

    def arrived(p, h):
        to_x(p, h).wait_recv()

    def from_partner(p):
        to_c(p, whole).wait_recv()

    def table_copy(k):
        peer = lax.rem(scen + k, n_scen)
        return pltpu.make_async_remote_copy(
            src_ref=tabs.at[scen], dst_ref=tabs.at[scen], send_sem=tsend.at[k], recv_sem=trecv.at[scen],
            device_id=(tm, peer), device_id_type=MESH)

    ids[...] = jnp.full(ids.shape, -1, jnp.int32)
    ids[0:1, :units] = ub_ref[...].reshape(1, units)
    ids[0:1, up:] = wb_ref[...].reshape(1, ids.shape[1] - up)
    step = 256
    number = lax.broadcasted_iota(jnp.int32, (step, ids.shape[1]), 0).astype(f32).astype(bf16)
    wanted = ids[0:1, :]
    one = jnp.ones((), bf16)
    for k in range(0, buses, step):
        here = jnp.where((wanted >= k) & (wanted < k + step), wanted - k, -1).astype(f32).astype(bf16)
        n = min(step, buses - k)
        hot[k:k + n, :] = jnp.where(number[:n] == here, one, one - one)
    tabs[scen] = jnp.concatenate(
        [tab_ref[...].astype(f32), jnp.broadcast_to(lim_ref[...].astype(f32).reshape(1, rows), (8, rows))], axis=0).astype(bf16)
    load_in[0].wait()

    def select(part_of):
        src = pl.ds(pl.multiple_of(part_of * 2 * quarter, 16), 2 * quarter)
        dst = pl.ds(pl.multiple_of(scen * rows + part_of * 2 * quarter, 16), 2 * quarter)
        fac[dst, :] = jnp.dot(fbuf[src, :], hot[...], preferred_element_type=f32).astype(bf16)

    select(y)
    pl.semaphore_wait(barrier, n_scen - 1 + n_tm - 1)

    p_own = piece(z, x, mine)

    def own_sends(f, parts):
        for h in parts:
            f(to_x(p_own, h))

            @pl.when(z > 0)
            def _():
                f(to_z(p_own, h, 0))

            @pl.when(z < n_z - 1)
            def _():
                f(to_z(p_own, h, 1))

    own_sends(lambda item: item.start(), range(2))
    for k in range(1, n_scen):
        table_copy(k).start()

    def edges_of(tile_last, tile_first):
        lane = lax.broadcasted_iota(jnp.int32, (up // 4, 128), 1)
        last = jnp.zeros((up // 4, 128), f32)
        first = jnp.zeros((up // 4, 128), f32)
        for g in range(4):
            inside = (lane >= 32 * g) & (lane < 32 * g + 32)
            a = tile_last[g * (up // 4):(g + 1) * (up // 4), :]
            b = tile_first[g * (up // 4):(g + 1) * (up // 4), :]
            sa = (32 * g - 96) % 128
            sb = (32 * g) % 128
            a = pltpu.roll(a, sa, 1) if sa else a
            b = pltpu.roll(b, sb, 1) if sb else b
            last = jnp.where(inside, a, last)
            first = jnp.where(inside, b, first)
        return last, first

    def edge_copy(number, way):
        dev = (tm + 1, scen) if way == 0 else (tm - 1, scen)
        return pltpu.make_async_remote_copy(
            src_ref=esend.at[number, way], dst_ref=erecv.at[number, way],
            send_sem=esem_s.at[number, way], recv_sem=esem_r.at[number, way],
            device_id=dev, device_id_type=MESH)

    def send_edges(number):
        last, first = edges_of(pw[:, cols - 128:], pw[:, :128])
        esend[number, 0] = last
        esend[number, 1] = first

        @pl.when(tm < n_tm - 1)
        def _():
            edge_copy(number, 0).start()

        @pl.when(tm > 0)
        def _():
            edge_copy(number, 1).start()

    def take_edges(number):
        @pl.when(tm > 0)
        def _():
            edge_copy(number, 0).wait_recv()
            e = erecv[number, 0]
            for g in range(4):
                s = (-32 * g) % 128
                bef[g * (up // 4):(g + 1) * (up // 4), :] = pltpu.roll(e, s, 1) if s else e

        @pl.when(tm == 0)
        def _():
            bef[...] = pw[:, :128]

        @pl.when(tm < n_tm - 1)
        def _():
            edge_copy(number, 1).wait_recv()
            e = erecv[number, 1]
            for g in range(4):
                s = (96 - 32 * g) % 128
                aft[g * (up // 4):(g + 1) * (up // 4), :] = pltpu.roll(e, s, 1) if s else e

        @pl.when(tm == n_tm - 1)
        def _():
            aft[...] = pw[:, cols - 128:]

    for item in load_in[1:]:
        item.wait()
    tail = jnp.zeros((up - units, cols), f32)
    pw[units:, :] = tail
    cm[units:, :] = tail
    mult[units:, :] = tail
    send_edges(0)
    select(oy)

    hour_row = lax.broadcasted_iota(jnp.int32, (2 * H_DEV, cols), 0)
    hour_col = lax.broadcasted_iota(jnp.int32, (2 * H_DEV, cols), 1)
    hour_of = ((hour_col >= hour_row * block) & (hour_col < hour_row * block + block)).astype(f32)
    load_of = hour_of.astype(bf16)
    bound_of = (hour_row == H_DEV).astype(f32).astype(bf16)
    lines_first = (((0,), (0,)), ((), ()))

    small[...] = jnp.zeros_like(small)
    small[:, :units] = cons_ref[...]
    target = jnp.dot(small[...].T, hour_of[:H_DEV], preferred_element_type=f32, precision=lax.Precision.HIGHEST)
    small[...] = jnp.zeros_like(small)
    small[:table_ref.shape[0], :units] = table_ref[...]
    table = small[...].T
    keep[...] = jnp.broadcast_to(1.0 - 2.0 * step_power * table[:, 1:2], keep.shape)
    lin[...] = jnp.broadcast_to(step_power * table[:, 0:1], lin.shape)
    cap[...] = jnp.broadcast_to(table[:, 2:3], cap.shape)
    ramp[...] = jnp.broadcast_to(table[:, 3:4], ramp.shape)
    off[...] = step_commit * (table[:, 4:5] + mult[...] - penalty * target)
    ext[:up, :] = pw[...].astype(bf16)
    needed = jnp.zeros((1, cols), f32)
    for h in range(H_DEV):
        needed = jnp.where(hour_of[h:h + 1] > 0.0, need_ref[h], needed)
    wind_row[...] = jnp.sum(ext[up:, :].astype(f32), axis=0, keepdims=True) - needed
    backs[...] = jnp.zeros((up, cols), f32)

    tile = 32
    lane = lax.broadcasted_iota(jnp.int32, (tile, half), 1)

    def start_next(r, p, both):
        capacity = cap[r, :]
        for i in range(2):
            h = pl.ds(i * half, half)
            commit = cm[r, h]
            short = jnp.maximum(p[i] - capacity * commit, 0.0)
            part[r, h] = p[i] * keep[r, :] - lin[r, :] - (step_power * short_weight) * short
            cm[r, h] = jnp.clip((1.0 - step_commit * penalty) * commit - off[r, h]
                                + (step_commit * short_weight) * capacity * short, 0.0, 1.0)

    def first_part(i, total):
        r = pl.ds(pl.multiple_of(i * tile, tile), tile)
        p = (pw[r, :half], pw[r, half:])
        start_next(r, p, True)
        both = jnp.concatenate(p, axis=1)
        return total + sum(both[8 * j:8 * j + 8] for j in range(tile // 8))

    def add_ramp(balance, first=0, last=up // tile):
        for i in range(first, last):
            r = pl.ds(i * tile, tile)
            p0, p1 = pw[r, :half], pw[r, half:]
            limit = ramp[r, :]
            r0, r1 = pltpu.roll(p0, block, 1), pltpu.roll(p1, block, 1)
            o0 = beyond(p0 - jnp.where(lane < block, p0, r0), limit)
            o1 = beyond(p1 - jnp.where(lane < block, r0, r1), limit)
            s0, s1 = pltpu.roll(o0, half - block, 1), pltpu.roll(o1, half - block, 1)
            f0 = jnp.where(lane >= half - block, s1, s0)
            f1 = jnp.where(lane >= half - block, 0.0, s1)
            part[r, :half] = part[r, :half] - (step_power * ramp_weight) * (o0 - f0) - balance[:, :half]
            part[r, half:] = part[r, half:] - (step_power * ramp_weight) * (o1 - f1) - balance[:, half:]

    def add_edges():
        for i in range(up // tile):
            r = pl.ds(i * tile, tile)
            limit = ramp[r, :]
            before = jnp.where(lane < block, beyond(pw[r, :half] - bef[r, :], limit), 0.0)
            after = jnp.where(lane >= half - block, beyond(aft[r, :] - pw[r, half:], limit), 0.0)
            part[r, :half] = part[r, :half] - (step_power * ramp_weight) * before
            part[r, half:] = part[r, half:] + (step_power * ramp_weight) * after

    def settle(last):
        def body(i, total):
            r = pl.ds(pl.multiple_of(i * tile, tile), tile)
            capacity = cap[r, :]
            p = []
            for j in range(2):
                h = pl.ds(j * half, half)
                p.append(jnp.minimum(jnp.maximum(part[r, h] - (step_power * flow_weight) * backs[r, h], 0.0), capacity))
                if last:
                    power_out_tile(r, h, p[j])
                else:
                    pw[r, h] = p[j]
                    ext[r, h] = p[j].astype(bf16)
            if last:
                return total
            start_next(r, p, True)
            both = jnp.concatenate(p, axis=1)
            return total + sum(both[8 * j:8 * j + 8] for j in range(tile // 8))
        return lax.fori_loop(0, up // tile, body, jnp.zeros((8, cols), f32), unroll=2)

    def power_out_tile(r, h, value):
        pw[r, h] = value

    def balance_of(total):
        return (step_power * balance_weight) * (jnp.sum(total, axis=0, keepdims=True) + wind_row[...])

    total = lax.fori_loop(0, up // tile, first_part, jnp.zeros((8, cols), f32), unroll=2)

    def line_step(at_rows):
        flows = jnp.dot(fac[at_rows, :], ext[...], preferred_element_type=f32) - load[at_rows, :]
        exc[at_rows, :] = beyond(flows, bound[at_rows, :]).astype(bf16)

    def process(zz):
        at_rows = pl.ds(pl.multiple_of(zz * chunk, 128), chunk)
        fact[:, at_rows] = fac[at_rows, :up].T
        line_step(at_rows)
        backs[...] += jnp.dot(fact[:, at_rows], exc[at_rows, :], preferred_element_type=f32)

    def table_arrived(src):
        pltpu.make_async_remote_copy(
            src_ref=tabs.at[src], dst_ref=tabs.at[src], send_sem=tsend.at[0], recv_sem=trecv.at[src],
            device_id=dev_x, device_id_type=MESH).wait_recv()

    def both(k, f, *rest):
        if k >= n_z:
            return

        @pl.when(z - k >= 0)
        def _():
            f(z - k, *rest)

        @pl.when(z + k < n_z)
        def _():
            f(z + k, *rest)

    def from_z(k, h):
        if k >= n_z:
            return
        for way in range(2):
            zz = z - k if way else z + k

            @pl.when(zz >= 0 if way else zz < n_z)
            def _():
                p = piece(zz, x, mine)
                arrived(p, h)

                @pl.when(z < n_z - 1 if way else z > 0)
                def _():
                    to_z(p, h, way).start()
                to_x(p, h).start()
                to_y(p, h).start()
                to_c(p, h).start()

    def from_xy(zz, h):
        p = piece(zz, ox, mine)
        arrived(p, h)

        @pl.when(c == 0)
        def _():
            to_y(p, h).start()
        to_c(p, h).start()
        p = piece(zz, x, other)
        arrived(p, h)

        @pl.when(c == 1)
        def _():
            to_x(p, h).start()
        to_c(p, h).start()

    def from_corner(zz, h):
        p = piece(zz, ox, other)
        arrived(p, h)
        to_c(p, h).start()

    def own_x(h):
        p = piece(z, ox, mine)
        arrived(p, h)
        to_y(p, h).start()
        to_c(p, h).start()

    def from_core(zz):
        for xx in range(2):
            for yy in range(2):
                from_partner(piece(zz, xx, yy * 2 + oc))
        process(zz)

    def own_chunk():
        for q in (oc, 2 + oc):
            from_partner(piece(z, ox, q))
        process(z)

    for h in range(2):
        own_x(h)
        from_z(1, h)
    take_edges(0)
    add_ramp(balance_of(total))
    add_edges()
    for k in range(1, n_scen):
        table_arrived(lax.rem(scen + k, n_scen))
    for s in range(n_scen):
        at_rows = pl.ds(s * rows, rows)
        load[at_rows, :] = lax.dot_general(tabs[s], load_of, lines_first, preferred_element_type=f32)
        bound[at_rows, :] = lax.dot_general(tabs[s], bound_of, lines_first, preferred_element_type=f32)
    for k in range(2, n_z + 2):
        for h in range(2):
            from_z(k, h)
            if k == 2:
                from_corner(z, h)
            both(k - 1, from_xy, h)
            if k > 2:
                both(k - 2, from_corner, h)
        if k == 3:
            own_chunk()
        if k > 3:
            both(k - 3, from_core)
    both(n_z - 1, from_core)

    total = settle(False)
    spread = hour_of[:H_DEV].astype(bf16)

    def sum_copy(k):
        return pltpu.make_async_remote_copy(
            src_ref=psend, dst_ref=precv.at[scen], send_sem=psem_s.at[k], recv_sem=psem_r.at[scen],
            device_id=(tm, lax.rem(scen + k, n_scen)), device_id_type=MESH)

    def put(i, src, dst):
        return pltpu.make_async_copy(src, dst, out_sem.at[i])

    put_commit = put(0, cm.at[pl.ds(0, units), :], commit_out)
    put_mult = put(1, mult.at[pl.ds(0, units), :], mult_out)
    put_power = put(2, pw.at[pl.ds(0, units), :], power_out)
    for number in range(1, PASSES):
        send_edges(number)
        final = number == PASSES - 1
        if final:
            put_commit.start()
            sums = jnp.zeros((H_DEV, up), f32)
            for item in split(cm[...] + mult[...] / penalty):
                sums = sums + lax.dot_general(spread, item, (((1,), (1,)), ((), ())), preferred_element_type=f32)
            psend[...] = sums
            for k in range(1, n_scen):
                sum_copy(k).start()
        balance = balance_of(total)
        tiles = up // tile
        for k in range(n_z):
            line_step(pl.ds(k * chunk, chunk))
            add_ramp(balance, tiles * k // n_z, tiles * (k + 1) // n_z)
        take_edges(number)
        add_edges()
        for m in range(2):
            r = pl.ds(m * (up // 2), up // 2)
            backs[r, :] = jnp.dot(fact[r, :], exc[...], preferred_element_type=f32)
        if final:
            precv[scen] = psend[...]
            for k in range(1, n_scen):
                src = lax.rem(scen + k, n_scen)
                pltpu.make_async_remote_copy(
                    src_ref=psend, dst_ref=precv.at[src], send_sem=psem_s.at[k], recv_sem=psem_r.at[src],
                    device_id=dev_x, device_id_type=MESH).wait_recv()
            totals = precv[0]
            for k in range(1, n_scen):
                totals = totals + precv[k]
            consensus = jnp.clip(totals / (block * n_scen), 0.0, 1.0)
            cons_out[...] = consensus[:, :units]
            pieces = jnp.concatenate([item.astype(f32) for item in split(consensus)], axis=0).T.astype(bf16)
            three = jnp.concatenate([hour_of[:H_DEV]] * 3, axis=0).astype(bf16)
            wide = jnp.dot(pieces, three, preferred_element_type=f32)
            mult[...] = mult[...] + penalty * (cm[...] - wide)
            put_mult.start()
        total = settle(final)
    put_power.start()

    own_sends(lambda item: item.wait_send(), (whole,))
    for h in (whole,):
        p = piece(z, ox, mine)
        to_y(p, h).wait_send()
        to_c(p, h).wait_send()
        to_c(piece(z, ox, other), h).wait_send()

    def drain(k, way):
        zz = z - k if way else z + k

        @pl.when(zz >= 0 if way else zz < n_z)
        def _():
            for h in (whole,):
                p = piece(zz, x, mine)

                @pl.when(z < n_z - 1 if way else z > 0)
                def _():
                    to_z(p, h, way).wait_send()
                to_x(p, h).wait_send()
                to_y(p, h).wait_send()
                to_c(p, h).wait_send()
                to_c(piece(zz, ox, mine), h).wait_send()
                to_c(piece(zz, x, other), h).wait_send()
                to_c(piece(zz, ox, other), h).wait_send()

                @pl.when(c == 0)
                def _():
                    to_y(piece(zz, ox, mine), h).wait_send()

                @pl.when(c == 1)
                def _():
                    to_x(piece(zz, x, other), h).wait_send()

    for k in range(1, n_z):
        for way in range(2):
            drain(k, way)
    for k in range(1, n_scen):
        table_copy(k).wait_send()
        sum_copy(k).wait_send()
    put_commit.wait()
    put_mult.wait()
    put_power.wait()
    for number in range(PASSES):
        @pl.when(tm < n_tm - 1)
        def _():
            edge_copy(number, 0).wait_send()

        @pl.when(tm > 0)
        def _():
            edge_copy(number, 1).wait_send()


def selection(unit_buses, wind_buses, buses, up, dtype):
    units = unit_buses.shape[0]
    wanted = jnp.concatenate([unit_buses, jnp.full((up - units,), -1, unit_buses.dtype), wind_buses])
    return (lax.broadcasted_iota(jnp.int32, (buses, wanted.shape[0]), 0) == wanted[None, :]).astype(dtype)


def finish(power_ref, commit_ref, mult_ref, cons_ref, power_out, commit_out, mult_out, cons_out):
    power_out[...] = power_ref[...]
    commit_out[...] = commit_ref[...]
    mult_out[...] = mult_ref[...]
    cons_out[...] = cons_ref[...]


def fused(n_tm, n_scen, prior_dispatch, prior_commitment, prior_consensus, prior_multiplier, flow_factors,
          unit_buses, wind_buses, wind_output, demand, load_flows, line_limits, unit_table):
    units, cols = prior_dispatch.shape
    rows, buses = flow_factors.shape
    farms = wind_output.shape[0]
    up = -(-units // 128) * 128
    f32, bf16 = jnp.float32, jnp.bfloat16
    lines = rows * n_scen
    wide = up + farms
    vm = pl.BlockSpec(memory_space=pltpu.VMEM)
    hbm = pl.BlockSpec(memory_space=pl.ANY)
    dma = pltpu.SemaphoreType.DMA
    shapes = (
        jax.ShapeDtypeStruct((units, cols), f32),
        jax.ShapeDtypeStruct((units, cols), f32),
        jax.ShapeDtypeStruct((units, cols), f32),
        jax.ShapeDtypeStruct((H_DEV, units), f32),
    )
    outs = pl.pallas_call(
        functools.partial(kernel, n_tm, n_scen, units),
        name="window",
        out_shape=shapes,
        in_specs=[hbm] * 5 + [vm] * 6 + [pl.BlockSpec(memory_space=pltpu.SMEM)],
        out_specs=(hbm, hbm, hbm, vm),
        scratch_shapes=[
            pltpu.VMEM((rows, buses), bf16),
            pltpu.VMEM((buses, wide), bf16),
            pltpu.VMEM((8, wide), jnp.int32),
            pltpu.VMEM((lines, wide), bf16),
            pltpu.VMEM((up, lines), bf16),
            pltpu.VMEM((lines, cols), f32),
            pltpu.VMEM((lines, cols), f32),
            pltpu.VMEM((lines, cols), bf16),
            pltpu.VMEM((up, cols), f32),
            pltpu.VMEM((up, cols), f32),
            pltpu.VMEM((up, cols), f32),
            pltpu.VMEM((up, cols), f32),
            pltpu.VMEM((up, cols), f32),
            pltpu.VMEM((wide, cols), bf16),
            pltpu.VMEM((up, cols), f32),
            pltpu.VMEM((up, 128), f32),
            pltpu.VMEM((up, 128), f32),
            pltpu.VMEM((up, 128), f32),
            pltpu.VMEM((up, 128), f32),
            pltpu.VMEM((up, 128), f32),
            pltpu.VMEM((up, 128), f32),
            pltpu.VMEM((n_scen, 2 * H_DEV, rows), bf16),
            pltpu.VMEM((PASSES, 2, up // 4, 128), f32),
            pltpu.VMEM((PASSES, 2, up // 4, 128), f32),
            pltpu.VMEM((H_DEV, up), f32),
            pltpu.VMEM((n_scen, H_DEV, up), f32),
            pltpu.VMEM((1, cols), f32),
            pltpu.VMEM((H_DEV, up), f32),
            dma((5,)),
            dma((3,)),
            dma((2, n_scen * 2)),
            dma((n_scen * 2,)),
            dma((2, n_scen // 2)),
            dma((n_scen,)),
            dma((n_scen,)),
            dma((n_scen * 2,)),
            dma((n_scen,)),
            dma((n_scen,)),
            dma((PASSES, 2)),
            dma((PASSES, 2)),
            dma((n_scen,)),
            dma((n_scen,)),
        ],
        compiler_params=pltpu.CompilerParams(collective_id=0, has_side_effects=True, vmem_limit_bytes=56 * 1024 * 1024),
    )(flow_factors, prior_dispatch, prior_commitment, prior_multiplier, wind_output,
      unit_buses, wind_buses, load_flows.T, line_limits,
      prior_consensus.T, unit_table, demand)
    power, commit, updated, cons = pl.pallas_call(
        finish,
        name="finish",
        out_shape=shapes,
        in_specs=[vm] * 4,
        out_specs=(vm,) * 4,
    )(*outs)
    return power, commit, cons.T, updated


def passed_along(value, axis, steps):
    count = lax.axis_size(axis)
    first, last = (max(0, -steps), min(count, count - steps))
    return lax.ppermute(value, axis, [(source, source + steps) for source in range(first, last)])


def plain(prior_dispatch, prior_commitment, prior_consensus, prior_multiplier, flow_factors,
          unit_buses, wind_buses, wind_output, demand, load_flows, line_limits, unit_table):
    units, columns = prior_dispatch.shape
    block = columns // H_DEV
    linear, quadratic, capacity, ramp_limit, noload = (unit_table[i][:, None] for i in range(5))
    factors = jnp.dot(flow_factors, selection(unit_buses, wind_buses, flow_factors.shape[1], units, jnp.bfloat16),
                      preferred_element_type=jnp.float32).astype(jnp.bfloat16)
    wind_total = jnp.sum(wind_output.astype(jnp.float32), axis=0)
    needed = jnp.repeat(demand, block)
    target = jnp.repeat(prior_consensus, block, axis=1)
    first_block = lax.axis_index("tm") == 0
    last_block = lax.axis_index("tm") == lax.axis_size("tm") - 1
    power, commit = prior_dispatch, prior_commitment
    factors = lax.all_gather(factors, "scen", axis=0, tiled=True)
    hourly = jnp.repeat(lax.all_gather(load_flows, "scen", axis=0, tiled=True).astype(jnp.float32), block, axis=1)
    limit = lax.all_gather(line_limits, "scen", axis=0, tiled=True).astype(jnp.float32)[:, None]
    for _ in range(PASSES):
        extended = jnp.concatenate([power.astype(jnp.bfloat16), wind_output], axis=0)
        flows = jnp.dot(factors, extended, preferred_element_type=jnp.float32) - hourly
        excess = (flows - jnp.clip(flows, -limit, limit)).astype(jnp.bfloat16)
        back = lax.dot_general(factors[:, :units], excess, (((0,), (0,)), ((), ())), preferred_element_type=jnp.float32)
        before = passed_along(power[:, columns - block:], "tm", 1)
        after = passed_along(power[:, :block], "tm", -1)
        before = jnp.where(first_block, power[:, :block], before)
        after = jnp.where(last_block, power[:, columns - block:], after)
        rate = power - jnp.concatenate([before, power[:, :columns - block]], axis=1)
        coming = jnp.concatenate([power[:, block:], after], axis=1) - power
        over = rate - jnp.clip(rate, -ramp_limit, ramp_limit)
        following = coming - jnp.clip(coming, -ramp_limit, ramp_limit)
        balance = jnp.sum(power, axis=0) + wind_total - needed
        short = jnp.maximum(power - capacity * commit, 0.0)
        grad_power = (linear + 2.0 * quadratic * power + flow_weight * back + ramp_weight * (over - following)
                      + balance_weight * balance + short_weight * short)
        grad_commit = noload - short_weight * capacity * short + prior_multiplier + penalty * (commit - target)
        power, commit = (jnp.clip(power - step_power * grad_power, 0.0, capacity),
                         jnp.clip(commit - step_commit * grad_commit, 0.0, 1.0))
    sums = jnp.sum((commit + prior_multiplier / penalty).reshape(units, H_DEV, block), axis=2)
    totals = lax.psum(sums, "scen")
    consensus = jnp.clip(totals / (block * lax.axis_size("scen")), 0.0, 1.0)
    updated = prior_multiplier + penalty * (commit - jnp.repeat(consensus, block, axis=1))
    return power, commit, consensus, updated


def solution(mesh):
    n_tm, n_scen = mesh.shape["tm"], mesh.shape["scen"]

    def per_device(*args):
        rows, cols = args[4].shape[0], args[0].shape[1]
        fits = (n_tm == 4 and n_scen % 2 == 0 and rows % 64 == 0 and cols == 256
                and args[7].shape[0] % 128 == 0 and args[0].shape[0] % 128 > 0)
        if fits:
            return fused(n_tm, n_scen, *args)
        return plain(*args)

    both_axes = P(None, ("tm", "scen"))
    in_specs = (both_axes, both_axes, P(None, "tm"), both_axes, P("scen", None), P(), P(), both_axes,
                P("tm"), P("scen", "tm"), P("scen"), P())
    out_specs = (both_axes, both_axes, P(None, "tm"), both_axes)
    return jax.shard_map(per_device, mesh=mesh, in_specs=in_specs, out_specs=out_specs, check_vma=False)
```
